32 devices in a mesh: gx: 8 (over y, x, core), gy: 4 (over z).
Axes of the slice: x: 2, y: 2, z: 4, core: 2. Of those that a mesh axis runs over, the one named last changes fastest.
Arguments:
- tiles: float32 [256, 5, 128, 128], P(('gx', 'gy')), may hold values from 0 to 0.003125
- cols: int32 [256, 5], P(('gx', 'gy')), may hold values from 0 to 17, as said below
- boundary: int32 [32, 2], P(('gx', 'gy')), may hold values from 0 to 7, as said below
- current: float32 [32768, 64], P(('gx', 'gy')), may hold values from -44 to 44
- previous: float32 [32768, 64], P(('gx', 'gy')), may hold values from -44 to 44
Outputs:
- filtered: float32 [32768, 64], P(('gx', 'gy'))
- gram: float32 [64, 64], replicated
The draws below stay inside these ranges and needn't reach their ends.
Inputs may be any that keep to these rules, and one draw needn't show every extreme that they name: `cols`: in each part, block row r has r in its first tile slot; each value from 8 up to the table's last entry occurs exactly once among the part's block rows. `boundary`: the 2 entries of a row are distinct block rows of the part.
All inputs are finite; a program needn't handle non-finite values.
Results may differ from the reference program's by a relative error of at most 0.0003.
Values sent between devices are 32-bit elements; how exact they have to be, the bound alone decides.
A program may use at most 64 MiB of HBM per device.

```python
import math
import jax
import jax.numpy as jnp
from jax import lax

BLK = 128
NV = 64
TPR = 5
S = 2
ITERS = 3
RB = 8
PARTS_X = 8
PARTS_Y = 4
BLOCKS = 256
ROWS = 32768


def draw_boundary(key, part):
    devices = PARTS_X * PARTS_Y
    keys = jax.random.split(key, devices)
    return jax.vmap(lambda single: jax.random.permutation(single, RB)[:S])(keys).astype(jnp.int32)


def draw_cols(key, part):
    devices = PARTS_X * PARTS_Y
    remote = (devices.bit_length() - 1) * S
    slots_all = RB * (TPR - 1)

    def one_part(single):
        first_key, second_key = jax.random.split(single)
        ranks = jax.random.permutation(first_key, slots_all).astype(jnp.int32)
        locals_drawn = jax.random.randint(second_key, (slots_all,), 0, RB).astype(jnp.int32)
        values = jnp.where(ranks < remote, RB + ranks, locals_drawn).reshape(RB, TPR - 1)
        diagonal = jnp.arange(RB, dtype=jnp.int32)[:, None]
        return jnp.concatenate([diagonal, values], axis=1)
    keys = jax.random.split(key, devices)
    return jax.vmap(one_part)(keys).reshape(devices * RB, TPR).astype(jnp.int32)


def draw_field(key):
    keys = jax.random.split(key, 3)
    ramp = 1.0 + 0.8 * jnp.arange(ROWS, dtype=jnp.float32)[:, None] / float(ROWS)
    column_scale = jnp.exp(jax.random.uniform(keys[2], (1, NV), jnp.float32, math.log(0.5), math.log(2.0)))
    values = jnp.clip(jax.random.normal(keys[0], (ROWS, NV), jnp.float32), -4.0, 4.0)
    row_scale = jnp.exp(jax.random.uniform(keys[1], (ROWS, 1), jnp.float32, math.log(0.3), math.log(3.0)))
    field = values * column_scale * row_scale * ramp
    return field.astype(jnp.float32)


def draw_current(key, part):
    return draw_field(jax.random.fold_in(key, 11))


def draw_previous(key, part):
    return draw_field(jax.random.fold_in(key, 23))


def block_scale(own_key, dims, pieces, low, largest):
    factor_of = 1.0
    for position, parts in pieces:
        steps = jax.random.uniform(jax.random.fold_in(jax.random.fold_in(own_key, 6), position), (parts,), jnp.float32, low / len(pieces), largest / len(pieces))
        factor_of = factor_of * jnp.repeat(jnp.exp(steps), dims[position] // parts).reshape((-1,) + (1,) * (len(dims) - 1 - position))
    return factor_of


def setup_inputs(seed: int = 0) -> dict:
    arg_keys = jax.random.split(jax.random.key(seed), 6)
    tiles = jnp.clip(0.003125 * jax.random.uniform(arg_keys[0], (BLOCKS, TPR, BLK, BLK), jnp.float32) ** block_scale(arg_keys[0], (BLOCKS, TPR, BLK, BLK), ((0, 32),), -0.2, 0.2), 0.0, 0.003125)
    cols = draw_cols(jax.random.fold_in(arg_keys[5], 71), 0)
    boundary = draw_boundary(jax.random.fold_in(arg_keys[5], 71), 0)
    current = draw_current(jax.random.fold_in(arg_keys[5], 71), 0)
    previous = draw_previous(jax.random.fold_in(arg_keys[5], 71), 0)
    return dict(tiles=tiles, cols=cols, boundary=boundary, current=current, previous=previous)


def reference(tiles, cols, boundary, current, previous):
    devices = PARTS_X * PARTS_Y
    nbits = devices.bit_length() - 1
    tile_parts = tiles.reshape(devices, RB, TPR, BLK, BLK)
    col_parts = cols.reshape(devices, RB, TPR)
    bit_values = jnp.left_shift(jnp.ones((nbits,), jnp.int32), jnp.arange(nbits, dtype=jnp.int32))

    def apply_operator(field):
        blocks = field.reshape(devices, RB, BLK, NV)

        def one_part(owner):
            partners = jnp.bitwise_xor(owner, bit_values).astype(jnp.int32)
            chosen = boundary[partners]
            ghosts = blocks[partners[:, None], chosen].reshape(nbits * S, BLK, NV)
            table = jnp.concatenate([blocks[owner], ghosts], axis=0)
            operands = table[col_parts[owner]]
            return jnp.einsum("rtij,rtjv->riv", tile_parts[owner], operands, precision=lax.Precision.HIGHEST)

        return lax.map(one_part, jnp.arange(devices, dtype=jnp.int32)).reshape(ROWS, NV)

    field = current
    older = previous
    for step in range(ITERS):
        product = apply_operator(field)
        nexter = (2.0 / 0.75) * (product - 0.25 * field) - older
        older = field
        field = nexter
    filtered = field
    gram = jnp.dot(filtered.T, filtered, precision=lax.Precision.HIGHEST, preferred_element_type=jnp.float32) / float(ROWS)
    return filtered, gram
```

```python
import functools

import jax
import jax.numpy as jnp
from jax import lax
from jax.experimental import pallas as pl
from jax.experimental.pallas import tpu as pltpu
from jax.sharding import PartitionSpec as P

ITERS = 3
MESH = pl.DeviceIdType.MESH


def contract(a, b):
    return lax.dot_general(a, b, (((1,), (1,)), ((), ())), preferred_element_type=jnp.float32)


def split(x):
    high = x.astype(jnp.bfloat16)
    return high, (x - high.astype(jnp.float32)).astype(jnp.bfloat16)


def kernel(
    size_x,
    size_y,
    total_rows,
    cols,
    boundary,
    tiles,
    current,
    previous,
    filtered,
    gram,
    raw,
    pairs,
    table,
    fields,
    outgoing,
    ghosts,
    terms_y,
    terms_x,
    tile_sem,
    send_sem,
    recv_sem,
    send_y,
    recv_y,
    send_x,
    recv_x,
):
    block_rows, per_row, block, _ = raw.shape
    vectors = fields.shape[2]
    shared = outgoing.shape[1]
    i = lax.axis_index("gx")
    j = lax.axis_index("gy")

    partners = []
    for axis, size, me in (("gy", size_y, j), ("gx", size_x, i)):
        for bit in range(size.bit_length() - 1):
            stride = 2**bit
            partners.append({axis: me + stride - 2 * stride * ((me // stride) % 2)})
    peers_y = [{"gy": (j + k) % size_y} for k in range(1, size_y)]
    peers_x = [{"gx": (i + k) % size_x} for k in range(1, size_x)]

    barrier = pltpu.get_barrier_semaphore()
    for peer in peers_y + peers_x:
        pl.semaphore_signal(barrier, inc=1, device_id=peer, device_id_type=MESH)

    loads = [pltpu.make_async_copy(tiles.at[r], raw.at[r], tile_sem.at[r]) for r in range(block_rows)]
    for load in loads:
        load.start()

    for r in range(block_rows):
        fields[0, r] = previous[:, r * block : (r + 1) * block]
        fields[1, r] = current[:, r * block : (r + 1) * block]
    for s in range(shared):
        outgoing[0, s] = fields[1, boundary[0, s]]

    pl.semaphore_wait(barrier, len(peers_y) + len(peers_x))

    def exchange(step):
        copies = []
        for b, partner in enumerate(partners):
            copies.append(
                pltpu.make_async_remote_copy(
                    src_ref=outgoing.at[step],
                    dst_ref=ghosts.at[step, b],
                    send_sem=send_sem.at[step, b],
                    recv_sem=recv_sem.at[step, b],
                    device_id=partner,
                    device_id_type=MESH,
                )
            )
        for copy in copies:
            copy.start()
        return copies

    def enter(entry, value):
        high, low = split(value)
        table[entry, :vectors, :] = high
        table[entry, vectors:, :] = low

    def advance(step, r):
        operand = jnp.concatenate([table[cols[r, t]] for t in range(per_row)], axis=1)
        parts = contract(operand, pairs[r])
        product = parts[:vectors, :block] + (parts[vectors:, :block] + parts[:vectors, block:])
        return 2.0 / 0.75 * (product - 0.25 * fields[step + 1, r]) - fields[step, r]

    copies = exchange(0)
    started = list(copies)
    for r in range(block_rows):
        enter(r, fields[1, r])
    for r in range(block_rows):
        loads[r].wait()
        for t in range(per_row):
            high, low = split(raw[r, t])
            pairs[r, :block, t * block : (t + 1) * block] = high
            pairs[r, block:, t * block : (t + 1) * block] = low

    for step in range(ITERS):
        for b, copy in enumerate(copies):
            copy.wait_recv()
            for s in range(shared):
                enter(block_rows + b * shared + s, ghosts[step, b, s])
        if step < ITERS - 1:
            for s in range(shared):
                outgoing[step + 1, s] = advance(step, boundary[0, s])
            copies = exchange(step + 1)
            started += copies
            for r in range(block_rows):
                fields[step + 2, r] = advance(step, r)
            for r in range(block_rows):
                enter(r, fields[step + 2, r])
        else:
            halves = []
            for r in range(block_rows):
                value = advance(step, r)
                filtered[:, r * block : (r + 1) * block] = value
                halves.append(jnp.concatenate(split(value), axis=0))
            whole = jnp.concatenate(halves, axis=1)
            parts = contract(whole, whole)
            total = parts[:vectors, :vectors] + (parts[vectors:, :vectors] + parts[:vectors, vectors:])

    half = vectors // 2

    def share(total, me, axis, peers, terms, send, recv):
        terms[me] = total
        moves = []
        for k, peer in enumerate(peers):
            moves.append(
                pltpu.make_async_remote_copy(
                    src_ref=terms.at[me],
                    dst_ref=terms.at[me],
                    send_sem=send.at[k],
                    recv_sem=recv.at[k],
                    device_id=peer,
                    device_id_type=MESH,
                )
            )
        for move in moves:
            move.start()
        for move in moves:
            move.wait_recv()
        result = terms[0]
        for k in range(1, terms.shape[0]):
            result = result + terms[k]
        return result, moves

    total = jnp.concatenate([total[:half], total[half:]], axis=1)
    total, moves = share(total, j, "gy", peers_y, terms_y, send_y, recv_y)
    started += moves
    total, moves = share(total, i, "gx", peers_x, terms_x, send_x, recv_x)
    started += moves
    total = total / float(total_rows)
    gram[:half, :] = total[:, :vectors]
    gram[half:, :] = total[:, vectors:]
    for copy in started:
        copy.wait_send()


def shards(tiles, cols, boundary, current, previous):
    size_x = lax.axis_size("gx")
    size_y = lax.axis_size("gy")
    block_rows, per_row, block, _ = tiles.shape
    rows, vectors = current.shape
    shared = boundary.shape[1]
    bits = (size_x * size_y).bit_length() - 1
    entries = block_rows + bits * shared
    vmem = pl.BlockSpec(memory_space=pltpu.VMEM)
    smem = pl.BlockSpec(memory_space=pltpu.SMEM)
    dma = pltpu.SemaphoreType.DMA
    filtered, gram = pl.pallas_call(
        functools.partial(kernel, size_x, size_y, rows * size_x * size_y),
        out_shape=(
            jax.ShapeDtypeStruct((vectors, rows), jnp.float32),
            jax.ShapeDtypeStruct((vectors, vectors), jnp.float32),
        ),
        in_specs=[smem, smem, pl.BlockSpec(memory_space=pl.ANY), vmem, vmem],
        out_specs=(vmem, vmem),
        scratch_shapes=[
            pltpu.VMEM(tiles.shape, jnp.float32),
            pltpu.VMEM((block_rows, 2 * block, per_row * block), jnp.bfloat16),
            pltpu.VMEM((entries, 2 * vectors, block), jnp.bfloat16),
            pltpu.VMEM((ITERS + 1, block_rows, vectors, block), jnp.float32),
            pltpu.VMEM((ITERS, shared, vectors, block), jnp.float32),
            pltpu.VMEM((ITERS, bits, shared, vectors, block), jnp.float32),
            pltpu.VMEM((size_y, vectors // 2, 2 * vectors), jnp.float32),
            pltpu.VMEM((size_x, vectors // 2, 2 * vectors), jnp.float32),
            dma((block_rows,)),
            dma((ITERS, bits)),
            dma((ITERS, bits)),
            dma((max(size_y - 1, 1),)),
            dma((max(size_y - 1, 1),)),
            dma((max(size_x - 1, 1),)),
            dma((max(size_x - 1, 1),)),
        ],
        compiler_params=pltpu.CompilerParams(
            collective_id=0, has_side_effects=True, vmem_limit_bytes=63 * 1024 * 1024
        ),
    )(cols, boundary, tiles, current.T, previous.T)
    return filtered.T, gram


def solution(mesh):
    in_specs = (
        P(("gx", "gy"), None, None, None),
        P(("gx", "gy"), None),
        P(("gx", "gy"), None),
        P(("gx", "gy"), None),
        P(("gx", "gy"), None),
    )
    out_specs = (P(("gx", "gy"), None), P())
    return jax.shard_map(shards, mesh=mesh, in_specs=in_specs, out_specs=out_specs, check_vma=False)
```

```python
import functools

import jax
import jax.numpy as jnp
from jax import lax
from jax.experimental import pallas as pl
from jax.experimental.pallas import tpu as pltpu
from jax.sharding import PartitionSpec as P

ITERS = 3
GROUPS = 2
STRIP = 8
MESH = pl.DeviceIdType.MESH


def contract(a, b):
    return lax.dot_general(a, b, (((1,), (1,)), ((), ())), preferred_element_type=jnp.float32)


def split(x):
    high = x.astype(jnp.bfloat16)
    return high, (x - high.astype(jnp.float32)).astype(jnp.bfloat16)


def kernel(
    size_x,
    size_y,
    paired,
    total_rows,
    cols_in,
    boundary_in,
    tiles,
    current,
    previous,
    filtered,
    gram,
    cols,
    boundary,
    now,
    before,
    raw,
    pairs,
    table,
    fields,
    outgoing,
    ghosts,
    mine,
    pieces,
    sums,
    whole,
    load_sem,
    send_sem,
    recv_sem,
    send_y,
    recv_y,
    send_x,
    recv_x,
    send_back,
    recv_back,
):
    block_rows, per_row, block, _ = raw.shape
    vectors = fields.shape[2]
    _, groups, shared, width, _ = outgoing.shape
    i = lax.axis_index("gx")
    j = lax.axis_index("gy")

    partners = []
    for axis, size, me in (("gy", size_y, j), ("gx", size_x, i)):
        for bit in range(size.bit_length() - 1):
            stride = 2**bit
            partners.append({axis: me + stride - 2 * stride * ((me // stride) % 2)})
    bits_low = size_y.bit_length() - 1
    order = list(reversed(range(bits_low))) + list(range(bits_low, len(partners)))
    peers_y = [(j + k) % size_y for k in range(1, size_y)]
    peers_x = [(i + k) % size_x for k in range(1, size_x)]
    if paired:
        buddy = {"gx": i + 1 - 2 * (i % 2), "gy": j}
        shifts = [(m, n) for m in range(size_x // 2) for n in range(size_y) if m or n]
        others = [{"gx": (i + 2 * m) % size_x, "gy": (j + n) % size_y} for m, n in shifts]
        greeted = others + [buddy]
    else:
        greeted = [{"gy": n} for n in peers_y] + [{"gx": n} for n in peers_x]

    barrier = pltpu.get_barrier_semaphore()
    for peer in greeted:
        pl.semaphore_signal(barrier, inc=1, device_id=peer, device_id_type=MESH)

    ends = [(boundary_in, boundary), (current, now), (cols_in, cols), (previous, before)]
    ends += [(tiles.at[r], raw.at[r]) for r in range(block_rows)]
    loads = [pltpu.make_async_copy(a, b, load_sem.at[n]) for n, (a, b) in enumerate(ends)]
    for load in loads:
        load.start()

    def exchange(step, g):
        copies = {}
        for b in order:
            copies[b] = pltpu.make_async_remote_copy(
                src_ref=outgoing.at[step, g],
                dst_ref=ghosts.at[step, g, b],
                send_sem=send_sem.at[step * groups + g, b],
                recv_sem=recv_sem.at[step * groups + g, b],
                device_id=partners[b],
                device_id_type=MESH,
            )
            copies[b].start()
        return copies

    def enter(entry, g, value):
        high, low = split(value)
        table[entry, 2 * g * width : (2 * g + 1) * width, :] = high
        table[entry, (2 * g + 1) * width : (2 * g + 2) * width, :] = low

    def advance(step, r, first, last):
        operand = jnp.concatenate(
            [table[cols[r, t], 2 * first * width : 2 * last * width, :] for t in range(per_row)], axis=1
        )
        parts = contract(operand, pairs[r])
        products = []
        for g in range(last - first):
            high = parts[2 * g * width : (2 * g + 1) * width]
            low = parts[(2 * g + 1) * width : (2 * g + 2) * width]
            products.append(high[:, :block] + (low[:, :block] + high[:, block:]))
        product = jnp.concatenate(products, axis=0)
        span = slice(first * width, last * width)
        return 2.0 / 0.75 * (product - 0.25 * fields[step + 1, r, span, :]) - fields[step, r, span, :]

    def part(g):
        return slice(g * width, (g + 1) * width)

    loads[0].wait()
    loads[1].wait()
    for r in range(block_rows):
        fields[1, r] = now[:, r * block : (r + 1) * block]
    for s in range(shared):
        for g in range(groups):
            outgoing[0, g, s] = fields[1, boundary[0, s], part(g), :]
    pl.semaphore_wait(barrier, len(greeted))
    flights = [exchange(0, g) for g in range(groups)]
    started = [copy for copies in flights for copy in copies.values()]

    for r in range(block_rows):
        for g in range(groups):
            enter(r, g, fields[1, r, part(g), :])
    loads[2].wait()
    loads[3].wait()
    for r in range(block_rows):
        fields[0, r] = before[:, r * block : (r + 1) * block]
    for r in range(block_rows):
        loads[4 + r].wait()
        for t in range(per_row):
            high, low = split(raw[r, t])
            pairs[r, :block, t * block : (t + 1) * block] = high
            pairs[r, block:, t * block : (t + 1) * block] = low

    for step in range(ITERS):
        for g in range(groups):
            for b in reversed(order):
                flights[g][b].wait_recv()
                for s in range(shared):
                    enter(block_rows + b * shared + s, g, ghosts[step, g, b, s])
            if step < ITERS - 1:
                for s in range(shared):
                    outgoing[step + 1, g, s] = advance(step, boundary[0, s], g, g + 1)
                flights[g] = exchange(step + 1, g)
                started += flights[g].values()
        if step < ITERS - 1:
            for r in range(block_rows):
                fields[step + 2, r] = advance(step, r, 0, groups)
            for r in range(block_rows):
                for g in range(groups):
                    enter(r, g, fields[step + 2, r, part(g), :])
        else:
            halves = []
            for r in range(block_rows):
                value = advance(step, r, 0, groups)
                filtered[:, r * block : (r + 1) * block] = value
                halves.append(jnp.concatenate(split(value), axis=0))
            rows = jnp.concatenate(halves, axis=1)
            parts = contract(rows, rows)
            total = parts[:vectors, :vectors] + (parts[vectors:, :vectors] + parts[:vectors, vectors:])

    half = vectors // 2

    def share(moves_of, send, recv):
        moves = []
        for k, (source, target, peer) in enumerate(moves_of):
            moves.append(
                pltpu.make_async_remote_copy(
                    src_ref=source,
                    dst_ref=target,
                    send_sem=send.at[k],
                    recv_sem=recv.at[k],
                    device_id=peer,
                    device_id_type=MESH,
                )
            )
            moves[-1].start()
        for move in moves:
            move.wait_recv()
        return moves

    def added(terms):
        result = terms[0]
        for k in range(1, terms.shape[0]):
            result = result + terms[k]
        return result

    if paired:
        side = i % 2
        pair = (i // 2) * size_y + j
        strips = half // STRIP
        row = lax.broadcasted_iota(jnp.int32, (half, half), 0)
        column = lax.broadcasted_iota(jnp.int32, (half, half), 1)
        corner = total[half:, half:]
        mixed = jnp.where(row <= column, total[:half, :half], corner)
        diagonal = jnp.sum(jnp.where(row == column, corner, 0.0), axis=0, keepdims=True)
        spare = mine.shape[2] - half

        def fold(value):
            return jnp.concatenate([value[n * STRIP : (n + 1) * STRIP] for n in range(strips)], axis=1)

        def unfold(value):
            return jnp.concatenate([value[:, n * half : (n + 1) * half] for n in range(strips)], axis=0)

        mine[0, :STRIP, :] = fold(total[:half, half:])
        mine[0, STRIP:, :] = jnp.zeros((1, half + spare), jnp.float32)
        mine[1, :STRIP, :] = fold(mixed)
        mine[1, STRIP:, :] = jnp.concatenate([diagonal, jnp.zeros((1, spare), jnp.float32)], axis=1)
        started += share([(mine.at[1 - side], pieces.at[0], buddy)], send_x, recv_x)
        sums[pair] = mine[side] + pieces[0]
        started += share([(sums.at[pair], sums.at[pair], peer) for peer in others], send_y, recv_y)
        whole[side] = added(sums) / float(total_rows)
        started += share([(whole.at[side], whole.at[side], buddy)], send_back, recv_back)
        right = unfold(whole[0, :STRIP, :])
        mixed = unfold(whole[1, :STRIP, :])
        flipped = mixed.T
        diagonal = whole[1, STRIP:, :half]
        gram[:half, :half] = jnp.where(row <= column, mixed, flipped)
        gram[:half, half:] = right
        gram[half:, :half] = right.T
        gram[half:, half:] = jnp.where(row > column, mixed, jnp.where(row < column, flipped, diagonal))
    else:
        total = jnp.concatenate([total[:half], total[half:]], axis=1)
        height = half // size_x
        for n in range(size_x):
            mine[n] = total[n * height : (n + 1) * height]
        pieces[i] = mine[i]
        started += share([(mine.at[n], pieces.at[i], {"gx": n}) for n in peers_x], send_x, recv_x)
        sums[j] = added(pieces)
        started += share([(sums.at[j], sums.at[j], {"gy": n}) for n in peers_y], send_y, recv_y)
        whole[i] = added(sums) / float(total_rows)
        started += share([(whole.at[i], whole.at[i], {"gx": n}) for n in peers_x], send_back, recv_back)
        for n in range(size_x):
            gram[n * height : (n + 1) * height, :] = whole[n][:, :vectors]
            gram[half + n * height : half + (n + 1) * height, :] = whole[n][:, vectors:]
    for copy in started:
        copy.wait_send()


def deliver(filtered_in, gram_in, filtered, gram, sems):
    moves = [
        pltpu.make_async_copy(filtered_in, filtered, sems.at[0]),
        pltpu.make_async_copy(gram_in, gram, sems.at[1]),
    ]
    for move in moves:
        move.start()
    for move in moves:
        move.wait()


def shards(tiles, cols, boundary, current, previous):
    size_x = lax.axis_size("gx")
    size_y = lax.axis_size("gy")
    block_rows, per_row, block, _ = tiles.shape
    rows, vectors = current.shape
    shared = boundary.shape[1]
    bits = (size_x * size_y).bit_length() - 1
    entries = block_rows + bits * shared
    width = vectors // GROUPS
    paired = size_x % 2 == 0 and size_x * size_y <= 64
    if paired:
        pairs = size_x // 2 * size_y
        piece = (STRIP + 1, vectors // 2 * (vectors // 2 // STRIP))
        counts = (2, 1, pairs, 2)
    else:
        piece = (vectors // 2 // size_x, 2 * vectors)
        counts = (size_x, size_x, size_y, size_x)
    vmem = pl.BlockSpec(memory_space=pltpu.VMEM)
    hbm = pl.BlockSpec(memory_space=pltpu.HBM)
    dma = pltpu.SemaphoreType.DMA
    filtered, gram = pl.pallas_call(
        functools.partial(kernel, size_x, size_y, paired, rows * size_x * size_y),
        out_shape=(
            pltpu.VMEM((vectors, rows), jnp.float32),
            pltpu.VMEM((vectors, vectors), jnp.float32),
        ),
        in_specs=[hbm] * 5,
        out_specs=(vmem, vmem),
        scratch_shapes=[
            pltpu.SMEM(cols.shape, jnp.int32),
            pltpu.SMEM(boundary.shape, jnp.int32),
            pltpu.VMEM((vectors, rows), jnp.float32),
            pltpu.VMEM((vectors, rows), jnp.float32),
            pltpu.VMEM(tiles.shape, jnp.float32),
            pltpu.VMEM((block_rows, 2 * block, per_row * block), jnp.bfloat16),
            pltpu.VMEM((entries, 2 * vectors, block), jnp.bfloat16),
            pltpu.VMEM((ITERS + 1, block_rows, vectors, block), jnp.float32),
            pltpu.VMEM((ITERS, GROUPS, shared, width, block), jnp.float32),
            pltpu.VMEM((ITERS, GROUPS, bits, shared, width, block), jnp.float32),
            *[pltpu.VMEM((count, *piece), jnp.float32) for count in counts],
            dma((4 + block_rows,)),
            dma((ITERS * GROUPS, bits)),
            dma((ITERS * GROUPS, bits)),
            *[dma((max(counts),)) for _ in range(6)],
        ],
        compiler_params=pltpu.CompilerParams(
            collective_id=0, has_side_effects=True, vmem_limit_bytes=63 * 1024 * 1024
        ),
    )(cols, boundary, tiles, current.T, previous.T)
    filtered, gram = pl.pallas_call(
        deliver,
        out_shape=(
            jax.ShapeDtypeStruct((vectors, rows), jnp.float32),
            jax.ShapeDtypeStruct((vectors, vectors), jnp.float32),
        ),
        in_specs=[vmem, vmem],
        out_specs=(hbm, hbm),
        scratch_shapes=[dma((2,))],
        compiler_params=pltpu.CompilerParams(vmem_limit_bytes=1024 * 1024),
    )(filtered, gram)
    return filtered.T, gram


def solution(mesh):
    in_specs = (
        P(("gx", "gy"), None, None, None),
        P(("gx", "gy"), None),
        P(("gx", "gy"), None),
        P(("gx", "gy"), None),
        P(("gx", "gy"), None),
    )
    out_specs = (P(("gx", "gy"), None), P())
    return jax.shard_map(shards, mesh=mesh, in_specs=in_specs, out_specs=out_specs, check_vma=False)
```

```python
import functools

import jax
import jax.numpy as jnp
from jax import lax
from jax.experimental import pallas as pl
from jax.experimental.pallas import tpu as pltpu
from jax.sharding import PartitionSpec as P

ITERS = 3
GROUPS = 2
STRIP = 8
MESH = pl.DeviceIdType.MESH


def contract(a, b):
    return lax.dot_general(a, b, (((1,), (1,)), ((), ())), preferred_element_type=jnp.float32)


def split(x):
    high = x.astype(jnp.bfloat16)
    return high, (x - high.astype(jnp.float32)).astype(jnp.bfloat16)


def kernel(
    size_x,
    size_y,
    paired,
    total_rows,
    cols_in,
    boundary_in,
    tiles,
    current,
    previous,
    filtered,
    gram,
    cols,
    boundary,
    now,
    before,
    raw,
    pairs,
    table,
    fields,
    outgoing,
    ghosts,
    mine,
    pieces,
    sums,
    whole,
    load_sem,
    send_sem,
    recv_sem,
    send_y,
    recv_y,
    send_x,
    recv_x,
    send_back,
    recv_back,
):
    block_rows, per_row, block, _ = raw.shape
    vectors = fields.shape[2]
    _, groups, shared, width, _ = outgoing.shape
    i = lax.axis_index("gx")
    j = lax.axis_index("gy")

    partners = []
    for axis, size, me in (("gy", size_y, j), ("gx", size_x, i)):
        for bit in range(size.bit_length() - 1):
            stride = 2**bit
            partners.append({axis: me + stride - 2 * stride * ((me // stride) % 2)})
    bits_low = size_y.bit_length() - 1
    order = list(reversed(range(bits_low))) + list(reversed(range(bits_low, len(partners))))
    peers_y = [(j + k) % size_y for k in range(1, size_y)]
    peers_x = [(i + k) % size_x for k in range(1, size_x)]
    if paired:
        buddy = {"gx": i + 1 - 2 * (i % 2), "gy": j}
        shifts = [(m, n) for m in range(size_x // 2) for n in range(size_y) if m or n]
        others = [{"gx": (i + 2 * m) % size_x, "gy": (j + n) % size_y} for m, n in shifts]
        greeted = partners
    else:
        greeted = [{"gy": n} for n in peers_y] + [{"gx": n} for n in peers_x]

    barrier = pltpu.get_barrier_semaphore()
    for peer in greeted:
        pl.semaphore_signal(barrier, inc=1, device_id=peer, device_id_type=MESH)

    ends = [(boundary_in, boundary), (current, now), (cols_in, cols), (previous, before)]
    ends += [(tiles.at[r], raw.at[r]) for r in range(block_rows)]
    loads = [pltpu.make_async_copy(a, b, load_sem.at[n]) for n, (a, b) in enumerate(ends)]
    for load in loads:
        load.start()

    def exchange(step, g):
        copies = {}
        for b in order:
            copies[b] = pltpu.make_async_remote_copy(
                src_ref=outgoing.at[step, g],
                dst_ref=ghosts.at[step, g, b],
                send_sem=send_sem.at[step * groups + g, b],
                recv_sem=recv_sem.at[step * groups + g, b],
                device_id=partners[b],
                device_id_type=MESH,
            )
            copies[b].start()
        return copies

    def enter(entry, g, value):
        high, low = split(value)
        table[entry, 2 * g * width : (2 * g + 1) * width, :] = high
        table[entry, (2 * g + 1) * width : (2 * g + 2) * width, :] = low

    def advance(step, r, first, last):
        operand = jnp.concatenate(
            [table[cols[r, t], 2 * first * width : 2 * last * width, :] for t in range(per_row)], axis=1
        )
        parts = contract(operand, pairs[r])
        products = []
        for g in range(last - first):
            high = parts[2 * g * width : (2 * g + 1) * width]
            low = parts[(2 * g + 1) * width : (2 * g + 2) * width]
            products.append(high[:, :block] + (low[:, :block] + high[:, block:]))
        product = jnp.concatenate(products, axis=0)
        span = slice(first * width, last * width)
        return 2.0 / 0.75 * (product - 0.25 * fields[step + 1, r, span, :]) - fields[step, r, span, :]

    def part(g):
        return slice(g * width, (g + 1) * width)

    loads[0].wait()
    loads[1].wait()
    for r in range(block_rows):
        fields[1, r] = now[:, r * block : (r + 1) * block]
    for s in range(shared):
        for g in range(groups):
            outgoing[0, g, s] = fields[1, boundary[0, s], part(g), :]
    pl.semaphore_wait(barrier, len(greeted))
    flights = [exchange(0, g) for g in range(groups)]
    started = [copy for copies in flights for copy in copies.values()]

    for r in range(block_rows):
        for g in range(groups):
            enter(r, g, fields[1, r, part(g), :])
    loads[2].wait()
    loads[3].wait()
    for r in range(block_rows):
        fields[0, r] = before[:, r * block : (r + 1) * block]
    for r in range(block_rows):
        loads[4 + r].wait()
        for t in range(per_row):
            high, low = split(raw[r, t])
            pairs[r, :block, t * block : (t + 1) * block] = high
            pairs[r, block:, t * block : (t + 1) * block] = low

    for step in range(ITERS):
        for g in range(groups):
            for b in reversed(order):
                flights[g][b].wait_recv()
                for s in range(shared):
                    enter(block_rows + b * shared + s, g, ghosts[step, g, b, s])
            if step < ITERS - 1:
                for s in range(shared):
                    outgoing[step + 1, g, s] = advance(step, boundary[0, s], g, g + 1)
                flights[g] = exchange(step + 1, g)
                started += flights[g].values()
        if step < ITERS - 1:
            for r in range(block_rows):
                fields[step + 2, r] = advance(step, r, 0, groups)
            for r in range(block_rows):
                for g in range(groups):
                    enter(r, g, fields[step + 2, r, part(g), :])
        else:
            halves = []
            for r in range(block_rows):
                value = advance(step, r, 0, groups)
                filtered[:, r * block : (r + 1) * block] = value
                halves.append(jnp.concatenate(split(value), axis=0))
            rows = jnp.concatenate(halves, axis=1)
            parts = contract(rows, rows)
            total = parts[:vectors, :vectors] + (parts[vectors:, :vectors] + parts[:vectors, vectors:])

    half = vectors // 2

    def share(moves_of, send, recv):
        moves = []
        for k, (source, target, peer) in enumerate(moves_of):
            moves.append(
                pltpu.make_async_remote_copy(
                    src_ref=source,
                    dst_ref=target,
                    send_sem=send.at[k],
                    recv_sem=recv.at[k],
                    device_id=peer,
                    device_id_type=MESH,
                )
            )
            moves[-1].start()
        for move in moves:
            move.wait_recv()
        return moves

    def added(terms):
        result = terms[0]
        for k in range(1, terms.shape[0]):
            result = result + terms[k]
        return result

    if paired:
        side = i % 2
        pair = (i // 2) * size_y + j
        strips = half // STRIP
        row = lax.broadcasted_iota(jnp.int32, (half, half), 0)
        column = lax.broadcasted_iota(jnp.int32, (half, half), 1)
        corner = total[half:, half:]
        mixed = jnp.where(row <= column, total[:half, :half], corner)
        diagonal = jnp.sum(jnp.where(row == column, corner, 0.0), axis=0, keepdims=True)
        spare = mine.shape[2] - half

        def fold(value):
            return jnp.concatenate([value[n * STRIP : (n + 1) * STRIP] for n in range(strips)], axis=1)

        def unfold(value):
            return jnp.concatenate([value[:, n * half : (n + 1) * half] for n in range(strips)], axis=0)

        mine[0, :STRIP, :] = fold(total[:half, half:])
        mine[0, STRIP:, :] = jnp.zeros((1, half + spare), jnp.float32)
        mine[1, :STRIP, :] = fold(mixed)
        mine[1, STRIP:, :] = jnp.concatenate([diagonal, jnp.zeros((1, spare), jnp.float32)], axis=1)
        started += share([(mine.at[1 - side], pieces.at[0], buddy)], send_x, recv_x)
        sums[pair] = mine[side] + pieces[0]
        started += share([(sums.at[pair], sums.at[pair], peer) for peer in others], send_y, recv_y)
        whole[side] = added(sums) / float(total_rows)
        started += share([(whole.at[side], whole.at[side], buddy)], send_back, recv_back)
        right = unfold(whole[0, :STRIP, :])
        mixed = unfold(whole[1, :STRIP, :])
        flipped = mixed.T
        diagonal = whole[1, STRIP:, :half]
        gram[:half, :half] = jnp.where(row <= column, mixed, flipped)
        gram[:half, half:] = right
        gram[half:, :half] = right.T
        gram[half:, half:] = jnp.where(row > column, mixed, jnp.where(row < column, flipped, diagonal))
    else:
        total = jnp.concatenate([total[:half], total[half:]], axis=1)
        height = half // size_x
        for n in range(size_x):
            mine[n] = total[n * height : (n + 1) * height]
        pieces[i] = mine[i]
        started += share([(mine.at[n], pieces.at[i], {"gx": n}) for n in peers_x], send_x, recv_x)
        sums[j] = added(pieces)
        started += share([(sums.at[j], sums.at[j], {"gy": n}) for n in peers_y], send_y, recv_y)
        whole[i] = added(sums) / float(total_rows)
        started += share([(whole.at[i], whole.at[i], {"gx": n}) for n in peers_x], send_back, recv_back)
        for n in range(size_x):
            gram[n * height : (n + 1) * height, :] = whole[n][:, :vectors]
            gram[half + n * height : half + (n + 1) * height, :] = whole[n][:, vectors:]
    for copy in started:
        copy.wait_send()


def deliver(filtered_in, gram_in, filtered, gram, sems):
    moves = [
        pltpu.make_async_copy(filtered_in, filtered, sems.at[0]),
        pltpu.make_async_copy(gram_in, gram, sems.at[1]),
    ]
    for move in moves:
        move.start()
    for move in moves:
        move.wait()


def shards(tiles, cols, boundary, current, previous):
    size_x = lax.axis_size("gx")
    size_y = lax.axis_size("gy")
    block_rows, per_row, block, _ = tiles.shape
    rows, vectors = current.shape
    shared = boundary.shape[1]
    bits = (size_x * size_y).bit_length() - 1
    entries = block_rows + bits * shared
    width = vectors // GROUPS
    paired = size_x % 2 == 0 and bits <= ITERS + 2
    if paired:
        pairs = size_x // 2 * size_y
        piece = (STRIP + 1, vectors // 2 * (vectors // 2 // STRIP))
        counts = (2, 1, pairs, 2)
    else:
        piece = (vectors // 2 // size_x, 2 * vectors)
        counts = (size_x, size_x, size_y, size_x)
    vmem = pl.BlockSpec(memory_space=pltpu.VMEM)
    hbm = pl.BlockSpec(memory_space=pltpu.HBM)
    dma = pltpu.SemaphoreType.DMA
    filtered, gram = pl.pallas_call(
        functools.partial(kernel, size_x, size_y, paired, rows * size_x * size_y),
        out_shape=(
            pltpu.VMEM((vectors, rows), jnp.float32),
            pltpu.VMEM((vectors, vectors), jnp.float32),
        ),
        in_specs=[hbm] * 5,
        out_specs=(vmem, vmem),
        scratch_shapes=[
            pltpu.SMEM(cols.shape, jnp.int32),
            pltpu.SMEM(boundary.shape, jnp.int32),
            pltpu.VMEM((vectors, rows), jnp.float32),
            pltpu.VMEM((vectors, rows), jnp.float32),
            pltpu.VMEM(tiles.shape, jnp.float32),
            pltpu.VMEM((block_rows, 2 * block, per_row * block), jnp.bfloat16),
            pltpu.VMEM((entries, 2 * vectors, block), jnp.bfloat16),
            pltpu.VMEM((ITERS + 1, block_rows, vectors, block), jnp.float32),
            pltpu.VMEM((ITERS, GROUPS, shared, width, block), jnp.float32),
            pltpu.VMEM((ITERS, GROUPS, bits, shared, width, block), jnp.float32),
            *[pltpu.VMEM((count, *piece), jnp.float32) for count in counts],
            dma((4 + block_rows,)),
            dma((ITERS * GROUPS, bits)),
            dma((ITERS * GROUPS, bits)),
            *[dma((max(counts),)) for _ in range(6)],
        ],
        compiler_params=pltpu.CompilerParams(
            collective_id=0, has_side_effects=True, vmem_limit_bytes=63 * 1024 * 1024
        ),
    )(cols, boundary, tiles, current.T, previous.T)
    filtered, gram = pl.pallas_call(
        deliver,
        out_shape=(
            jax.ShapeDtypeStruct((vectors, rows), jnp.float32),
            jax.ShapeDtypeStruct((vectors, vectors), jnp.float32),
        ),
        in_specs=[vmem, vmem],
        out_specs=(hbm, hbm),
        scratch_shapes=[dma((2,))],
        compiler_params=pltpu.CompilerParams(vmem_limit_bytes=1024 * 1024),
    )(filtered, gram)
    return filtered.T, gram


def solution(mesh):
    in_specs = (
        P(("gx", "gy"), None, None, None),
        P(("gx", "gy"), None),
        P(("gx", "gy"), None),
        P(("gx", "gy"), None),
        P(("gx", "gy"), None),
    )
    out_specs = (P(("gx", "gy"), None), P())
    return jax.shard_map(shards, mesh=mesh, in_specs=in_specs, out_specs=out_specs, check_vma=False)
```

```python
import functools

import jax
import jax.numpy as jnp
from jax import lax
from jax.experimental import pallas as pl
from jax.experimental.pallas import tpu as pltpu
from jax.sharding import PartitionSpec as P

ITERS = 3
GROUPS = 2
STRIP = 8
MESH = pl.DeviceIdType.MESH


def contract(a, b):
    return lax.dot_general(a, b, (((1,), (1,)), ((), ())), preferred_element_type=jnp.float32)


def split(x):
    high = x.astype(jnp.bfloat16)
    return high, (x - high.astype(jnp.float32)).astype(jnp.bfloat16)


def kernel(
    size_x,
    size_y,
    paired,
    total_rows,
    cols_in,
    boundary_in,
    tiles,
    current,
    previous,
    filtered,
    gram,
    cols,
    boundary,
    now,
    before,
    raw,
    pairs,
    table,
    fields,
    outgoing,
    ghosts,
    mine,
    pieces,
    sums,
    whole,
    load_sem,
    send_sem,
    recv_sem,
    send_y,
    recv_y,
    send_x,
    recv_x,
    send_back,
    recv_back,
):
    block_rows, per_row, block, _ = raw.shape
    vectors = fields.shape[2]
    _, groups, shared, width, _ = outgoing.shape
    i = lax.axis_index("gx")
    j = lax.axis_index("gy")

    partners = []
    for axis, size, me in (("gy", size_y, j), ("gx", size_x, i)):
        for bit in range(size.bit_length() - 1):
            stride = 2**bit
            partners.append({axis: me + stride - 2 * stride * ((me // stride) % 2)})
    bits_low = size_y.bit_length() - 1
    order = list(reversed(range(bits_low))) + list(reversed(range(bits_low, len(partners))))
    peers_y = [(j + k) % size_y for k in range(1, size_y)]
    peers_x = [(i + k) % size_x for k in range(1, size_x)]
    if paired:
        buddy = {"gx": i + 1 - 2 * (i % 2), "gy": j}
        shifts = [(m, n) for m in reversed(range(size_x // 2)) for n in reversed(range(size_y)) if m or n]
        others = [{"gx": (i + 2 * m) % size_x, "gy": (j + n) % size_y} for m, n in shifts]
        greeted = partners
    else:
        greeted = [{"gy": n} for n in peers_y] + [{"gx": n} for n in peers_x]

    barrier = pltpu.get_barrier_semaphore()
    for peer in greeted:
        pl.semaphore_signal(barrier, inc=1, device_id=peer, device_id_type=MESH)

    ends = [(boundary_in, boundary), (current, now), (cols_in, cols), (previous, before)]
    ends += [(tiles.at[r], raw.at[r]) for r in range(block_rows)]
    loads = [pltpu.make_async_copy(a, b, load_sem.at[n]) for n, (a, b) in enumerate(ends)]
    for load in loads:
        load.start()

    def exchange(step, g):
        copies = {}
        for b in order:
            copies[b] = pltpu.make_async_remote_copy(
                src_ref=outgoing.at[step, g],
                dst_ref=ghosts.at[step, g, b],
                send_sem=send_sem.at[step * groups + g, b],
                recv_sem=recv_sem.at[step * groups + g, b],
                device_id=partners[b],
                device_id_type=MESH,
            )
            copies[b].start()
        return copies

    def enter(entry, g, value):
        high, low = split(value)
        table[entry, 2 * g * width : (2 * g + 1) * width, :] = high
        table[entry, (2 * g + 1) * width : (2 * g + 2) * width, :] = low

    def advance(step, r, first, last):
        operand = jnp.concatenate(
            [table[cols[r, t], 2 * first * width : 2 * last * width, :] for t in range(per_row)], axis=1
        )
        parts = contract(operand, pairs[r])
        products = []
        for g in range(last - first):
            high = parts[2 * g * width : (2 * g + 1) * width]
            low = parts[(2 * g + 1) * width : (2 * g + 2) * width]
            products.append(high[:, :block] + (low[:, :block] + high[:, block:]))
        product = jnp.concatenate(products, axis=0)
        span = slice(first * width, last * width)
        return 2.0 / 0.75 * (product - 0.25 * fields[step + 1, r, span, :]) - fields[step, r, span, :]

    def part(g):
        return slice(g * width, (g + 1) * width)

    loads[0].wait()
    loads[1].wait()
    for r in range(block_rows):
        fields[1, r] = now[:, r * block : (r + 1) * block]
    for s in range(shared):
        for g in range(groups):
            outgoing[0, g, s] = fields[1, boundary[0, s], part(g), :]
    pl.semaphore_wait(barrier, len(greeted))
    flights = [exchange(0, g) for g in range(groups)]
    started = [copy for copies in flights for copy in copies.values()]

    for r in range(block_rows):
        for g in range(groups):
            enter(r, g, fields[1, r, part(g), :])
    loads[2].wait()
    loads[3].wait()
    for r in range(block_rows):
        fields[0, r] = before[:, r * block : (r + 1) * block]
    for r in range(block_rows):
        loads[4 + r].wait()
        for t in range(per_row):
            high, low = split(raw[r, t])
            pairs[r, :block, t * block : (t + 1) * block] = high
            pairs[r, block:, t * block : (t + 1) * block] = low

    last = []
    for step in range(ITERS):
        for g in range(groups):
            for b in reversed(order):
                flights[g][b].wait_recv()
                for s in range(shared):
                    enter(block_rows + b * shared + s, g, ghosts[step, g, b, s])
            if step < ITERS - 1:
                for s in range(shared):
                    outgoing[step + 1, g, s] = advance(step, boundary[0, s], g, g + 1)
                flights[g] = exchange(step + 1, g)
                started += flights[g].values()
            else:
                last.append([advance(step, r, g, g + 1) for r in range(block_rows)])
        if step < ITERS - 1:
            for r in range(block_rows):
                fields[step + 2, r] = advance(step, r, 0, groups)
            for r in range(block_rows):
                for g in range(groups):
                    enter(r, g, fields[step + 2, r, part(g), :])
        else:
            halves = []
            for r in range(block_rows):
                value = jnp.concatenate([values[r] for values in last], axis=0)
                filtered[:, r * block : (r + 1) * block] = value
                halves.append(jnp.concatenate(split(value), axis=0))
            rows = jnp.concatenate(halves, axis=1)
            parts = contract(rows, rows)
            total = parts[:vectors, :vectors] + (parts[vectors:, :vectors] + parts[:vectors, vectors:])

    half = vectors // 2

    def share(moves_of, send, recv):
        moves = []
        for k, (source, target, peer) in enumerate(moves_of):
            moves.append(
                pltpu.make_async_remote_copy(
                    src_ref=source,
                    dst_ref=target,
                    send_sem=send.at[k],
                    recv_sem=recv.at[k],
                    device_id=peer,
                    device_id_type=MESH,
                )
            )
            moves[-1].start()
        for move in moves:
            move.wait_recv()
        return moves

    def added(terms):
        result = terms[0]
        for k in range(1, terms.shape[0]):
            result = result + terms[k]
        return result

    if paired:
        side = i % 2
        pair = (i // 2) * size_y + j
        strips = half // STRIP
        row = lax.broadcasted_iota(jnp.int32, (half, half), 0)
        column = lax.broadcasted_iota(jnp.int32, (half, half), 1)
        corner = total[half:, half:]
        mixed = jnp.where(row <= column, total[:half, :half], corner)
        diagonal = jnp.sum(jnp.where(row == column, corner, 0.0), axis=0, keepdims=True)
        spare = mine.shape[2] - half

        def fold(value):
            return jnp.concatenate([value[n * STRIP : (n + 1) * STRIP] for n in range(strips)], axis=1)

        def unfold(value):
            return jnp.concatenate([value[:, n * half : (n + 1) * half] for n in range(strips)], axis=0)

        mine[0, :STRIP, :] = fold(total[:half, half:])
        mine[0, STRIP:, :] = jnp.zeros((1, half + spare), jnp.float32)
        mine[1, :STRIP, :] = fold(mixed)
        mine[1, STRIP:, :] = jnp.concatenate([diagonal, jnp.zeros((1, spare), jnp.float32)], axis=1)
        started += share([(mine.at[1 - side], pieces.at[0], buddy)], send_x, recv_x)
        sums[pair] = mine[side] + pieces[0]
        started += share([(sums.at[pair], sums.at[pair], peer) for peer in others], send_y, recv_y)
        whole[side] = added(sums) / float(total_rows)
        started += share([(whole.at[side], whole.at[side], buddy)], send_back, recv_back)
        right = unfold(whole[0, :STRIP, :])
        mixed = unfold(whole[1, :STRIP, :])
        flipped = mixed.T
        diagonal = whole[1, STRIP:, :half]
        gram[:half, :half] = jnp.where(row <= column, mixed, flipped)
        gram[:half, half:] = right
        gram[half:, :half] = right.T
        gram[half:, half:] = jnp.where(row > column, mixed, jnp.where(row < column, flipped, diagonal))
    else:
        total = jnp.concatenate([total[:half], total[half:]], axis=1)
        height = half // size_x
        for n in range(size_x):
            mine[n] = total[n * height : (n + 1) * height]
        pieces[i] = mine[i]
        started += share([(mine.at[n], pieces.at[i], {"gx": n}) for n in peers_x], send_x, recv_x)
        sums[j] = added(pieces)
        started += share([(sums.at[j], sums.at[j], {"gy": n}) for n in peers_y], send_y, recv_y)
        whole[i] = added(sums) / float(total_rows)
        started += share([(whole.at[i], whole.at[i], {"gx": n}) for n in peers_x], send_back, recv_back)
        for n in range(size_x):
            gram[n * height : (n + 1) * height, :] = whole[n][:, :vectors]
            gram[half + n * height : half + (n + 1) * height, :] = whole[n][:, vectors:]
    for copy in started:
        copy.wait_send()


def deliver(filtered_in, gram_in, filtered, gram, sems):
    moves = [
        pltpu.make_async_copy(filtered_in, filtered, sems.at[0]),
        pltpu.make_async_copy(gram_in, gram, sems.at[1]),
    ]
    for move in moves:
        move.start()
    for move in moves:
        move.wait()


def shards(tiles, cols, boundary, current, previous):
    size_x = lax.axis_size("gx")
    size_y = lax.axis_size("gy")
    block_rows, per_row, block, _ = tiles.shape
    rows, vectors = current.shape
    shared = boundary.shape[1]
    bits = (size_x * size_y).bit_length() - 1
    entries = block_rows + bits * shared
    width = vectors // GROUPS
    paired = size_x % 2 == 0 and bits <= ITERS + 2
    if paired:
        pairs = size_x // 2 * size_y
        piece = (STRIP + 1, vectors // 2 * (vectors // 2 // STRIP))
        counts = (2, 1, pairs, 2)
    else:
        piece = (vectors // 2 // size_x, 2 * vectors)
        counts = (size_x, size_x, size_y, size_x)
    vmem = pl.BlockSpec(memory_space=pltpu.VMEM)
    hbm = pl.BlockSpec(memory_space=pltpu.HBM)
    dma = pltpu.SemaphoreType.DMA
    filtered, gram = pl.pallas_call(
        functools.partial(kernel, size_x, size_y, paired, rows * size_x * size_y),
        out_shape=(
            pltpu.VMEM((vectors, rows), jnp.float32),
            pltpu.VMEM((vectors, vectors), jnp.float32),
        ),
        in_specs=[hbm] * 5,
        out_specs=(vmem, vmem),
        scratch_shapes=[
            pltpu.SMEM(cols.shape, jnp.int32),
            pltpu.SMEM(boundary.shape, jnp.int32),
            pltpu.VMEM((vectors, rows), jnp.float32),
            pltpu.VMEM((vectors, rows), jnp.float32),
            pltpu.VMEM(tiles.shape, jnp.float32),
            pltpu.VMEM((block_rows, 2 * block, per_row * block), jnp.bfloat16),
            pltpu.VMEM((entries, 2 * vectors, block), jnp.bfloat16),
            pltpu.VMEM((ITERS + 1, block_rows, vectors, block), jnp.float32),
            pltpu.VMEM((ITERS, GROUPS, shared, width, block), jnp.float32),
            pltpu.VMEM((ITERS, GROUPS, bits, shared, width, block), jnp.float32),
            *[pltpu.VMEM((count, *piece), jnp.float32) for count in counts],
            dma((4 + block_rows,)),
            dma((ITERS * GROUPS, bits)),
            dma((ITERS * GROUPS, bits)),
            *[dma((max(counts),)) for _ in range(6)],
        ],
        compiler_params=pltpu.CompilerParams(
            collective_id=0, has_side_effects=True, vmem_limit_bytes=63 * 1024 * 1024
        ),
    )(cols, boundary, tiles, current.T, previous.T)
    filtered, gram = pl.pallas_call(
        deliver,
        out_shape=(
            jax.ShapeDtypeStruct((vectors, rows), jnp.float32),
            jax.ShapeDtypeStruct((vectors, vectors), jnp.float32),
        ),
        in_specs=[vmem, vmem],
        out_specs=(hbm, hbm),
        scratch_shapes=[dma((2,))],
        compiler_params=pltpu.CompilerParams(vmem_limit_bytes=1024 * 1024),
    )(filtered, gram)
    return filtered.T, gram


def solution(mesh):
    in_specs = (
        P(("gx", "gy"), None, None, None),
        P(("gx", "gy"), None),
        P(("gx", "gy"), None),
        P(("gx", "gy"), None),
        P(("gx", "gy"), None),
    )
    out_specs = (P(("gx", "gy"), None), P())
    return jax.shard_map(shards, mesh=mesh, in_specs=in_specs, out_specs=out_specs, check_vma=False)
```
